32 devices in a mesh: gx: 8 (over y, x, core), gy: 4 (over z).
Axes of the slice: x: 2, y: 2, z: 4, core: 2. Of those that a mesh axis runs over, the one named last changes fastest.
Arguments:
- quotient_table: float32 [32768, 256], P(('gx', 'gy')), may hold values from -6 to 6
- quotient_acc: float32 [32768, 256], P(('gx', 'gy')), may hold values from 1 to 64
- remainder_table: float32 [4096, 256], replicated, may hold values from -6 to 6
- remainder_acc: float32 [4096, 256], P(('gx', 'gy')), may hold values from 1 to 64
- cotangent: bfloat16 [2048, 256], P(('gx', 'gy')), may hold values from -6 to 6
- quotient_ids: int32 [2048, 20], P(('gx', 'gy')), may hold values from 0 to 32767, as said below
- remainder_ids: int32 [2048, 20], P(('gx', 'gy')), may hold values from 0 to 4095
Outputs:
- new_quotient: float32 [32768, 256], P(('gx', 'gy'))
- new_quotient_acc: float32 [32768, 256], P(('gx', 'gy'))
- new_remainder: float32 [4096, 256], replicated
- new_remainder_acc: float32 [4096, 256], P(('gx', 'gy'))
The draws below stay inside these ranges and needn't reach their ends.
Inputs may be any that keep to these rules, and one draw needn't show every extreme that they name: `quotient_ids`: call the rows k * 1024 to (k + 1) * 1024 - 1 the range of device k along gx+gy. Of the ids of one device's 64 samples, at most 80 fall in any one range; in every draw some range receives exactly 80 from every device.
All inputs are finite; a program needn't handle non-finite values.
Results may differ from the reference program's by a relative error of at most 0.0046.
Values may be sent and summed in bfloat16 or wider, within the bound.
A program may use at most 64 MiB of HBM per device.

```python
import math
import jax
import jax.numpy as jnp
from jax import lax

E = 256
R_ROWS = 4096
Q_DEV = 1024
B_DEV = 64
BAG = 20
SAMPLES = 2048
Q_ROWS = 32768
CAP = 80


def draw_quotient_ids(key, part):
    devices = SAMPLES // B_DEV
    lookups = B_DEV * BAG
    table_slots = devices * CAP
    noise_top = max(1, 2 ** 24 // table_slots)
    global_key, blocks_key = jax.random.split(jax.random.fold_in(key, 17))
    preferred_rows = jax.random.randint(global_key, (), 0, devices, dtype=jnp.int32)
    slot_owner_device = jnp.arange(table_slots, dtype=jnp.int32) // CAP

    def one_block(block_key):
        key_rank, key_noise, key_coin, key_order, key_rows = jax.random.split(block_key, 5)
        ranking = jax.random.permutation(key_rank, devices).astype(jnp.int32)
        popularity_rank = ranking[slot_owner_device]
        random_jitter = jax.random.randint(key_noise, (table_slots,), 0, noise_top, dtype=jnp.int32)
        random_toss = jax.random.randint(key_coin, (table_slots,), 0, 2, dtype=jnp.int32)
        priority_boost = jnp.where(slot_owner_device == preferred_rows, 2 ** 26, jnp.where(popularity_rank < 8, random_toss * 2 ** 25, 0))
        ranking_score = (priority_boost + random_jitter * table_slots + jnp.arange(table_slots, dtype=jnp.int32)).astype(jnp.int32)
        _, chosen = lax.top_k(ranking_score, lookups)
        owners = jax.random.permutation(key_order, slot_owner_device[chosen])
        rows = jax.random.randint(key_rows, (lookups,), 0, Q_DEV, dtype=jnp.int32)
        return owners * Q_DEV + rows
    block_keys = jax.random.split(blocks_key, devices)
    return jax.vmap(one_block)(block_keys).reshape(SAMPLES, BAG).astype(jnp.int32)


def place_ends(result, stream_key, smallest, largest):
    extent = result.shape
    index_at = [jax.random.randint(jax.random.fold_in(stream_key, axis), (), 0, extent[axis]) for axis in range(len(extent))]
    result = result.at[tuple(index_at)].set(smallest)
    longest = extent.index(max(extent))
    index_at[longest] = (index_at[longest] + 1) % extent[longest]
    return result.at[tuple(index_at)].set(largest)


def level_of(own_key, dims, cuts, least, top_value):
    gain, own = 1.0, jax.random.fold_in(own_key, 6)
    for position, parts in cuts:
        heights = jnp.exp(jax.random.uniform(jax.random.fold_in(own, position), (parts,), jnp.float32, least / len(cuts), top_value / len(cuts)))
        gain = gain * jnp.repeat(heights, dims[position] // parts).reshape([-1 if axis == position else 1 for axis in range(len(dims))])
    return gain


def noise(rng, extent, spread, limit, shards=(), held_as=jnp.bfloat16):
    entries = spread * jax.random.normal(rng, extent, jnp.float32)
    if shards:
        entries = entries * level_of(rng, extent, shards, -0.22, 0.18)
    return jnp.clip(entries, -limit, limit).astype(held_as)


def setup_inputs(seed: int = 0) -> dict:
    arg_keys = jax.random.split(jax.random.key(seed), 8)
    quotient_table = noise(arg_keys[0], (Q_ROWS, E), 1.0, 6.0, ((0, 32),), jnp.float32)
    quotient_acc = jnp.clip(jnp.exp(math.log(64.0) - 4.158883 * jax.random.uniform(arg_keys[1], (Q_ROWS, E), jnp.float32) ** level_of(arg_keys[1], (Q_ROWS, E), ((0, 32),), -0.2, 0.2)), 1.0, 64.0)
    remainder_table = noise(arg_keys[2], (R_ROWS, E), 1.0, 6.0, (), jnp.float32)
    remainder_acc = jnp.clip(jnp.exp(math.log(64.0) - 4.158883 * jax.random.uniform(arg_keys[3], (R_ROWS, E), jnp.float32) ** level_of(arg_keys[3], (R_ROWS, E), ((0, 32),), -0.2, 0.2)), 1.0, 64.0)
    cotangent = noise(arg_keys[4], (SAMPLES, E), 1.0, 6.0, ((0, 32),))
    quotient_ids = draw_quotient_ids(jax.random.fold_in(arg_keys[7], 71), 0)
    remainder_ids = place_ends(jax.random.randint(arg_keys[6], (SAMPLES, BAG), 0, R_ROWS), jax.random.fold_in(arg_keys[6], 1), 0, R_ROWS - 1).astype(jnp.int32)
    return {"quotient_table": quotient_table, "quotient_acc": quotient_acc, "remainder_table": remainder_table, "remainder_acc": remainder_acc, "cotangent": cotangent, "quotient_ids": quotient_ids, "remainder_ids": remainder_ids}


LEARNING_RATE = 0.1
EPSILON = 1e-10

def adagrad(param, accum, grad):
    fresh = accum + grad * grad
    return (param - LEARNING_RATE * grad / (jnp.sqrt(fresh) + EPSILON), fresh)

def reference(quotient_table, quotient_acc, remainder_table, remainder_acc, cotangent, quotient_ids, remainder_ids):
    bag = quotient_ids.shape[1]
    flat_q = quotient_ids.reshape(-1).astype(jnp.int32)
    flat_r = remainder_ids.reshape(-1).astype(jnp.int32)
    cot_rows = jnp.repeat(cotangent, bag, axis=0).astype(jnp.float32)
    q_rows = lax.optimization_barrier(quotient_table[flat_q].astype(jnp.bfloat16))
    r_rows = lax.optimization_barrier(remainder_table[flat_r].astype(jnp.bfloat16))
    q_terms = (cot_rows * r_rows.astype(jnp.float32)).astype(jnp.bfloat16)
    r_terms = (cot_rows * q_rows.astype(jnp.float32)).astype(jnp.bfloat16)
    quotient_grad = jax.ops.segment_sum(q_terms.astype(jnp.float32), flat_q, num_segments=Q_ROWS)
    remainder_grad = jax.ops.segment_sum(r_terms.astype(jnp.float32), flat_r, num_segments=R_ROWS)
    new_quotient, new_quotient_acc = adagrad(quotient_table, quotient_acc, quotient_grad)
    new_remainder, new_remainder_acc = adagrad(remainder_table, remainder_acc, remainder_grad)
    return (new_quotient, new_quotient_acc, new_remainder, new_remainder_acc)
```

```python
import functools

import jax
import jax.numpy as jnp
from jax import lax
from jax.experimental import pallas as pl
from jax.experimental.pallas import tpu as pltpu
from jax.sharding import PartitionSpec as P

LEARNING_RATE = 0.1
EPSILON = 1e-10
MESH = pl.DeviceIdType.MESH
VMEM = pltpu.VMEM


def adagrad(param, accum, grad):
    fresh = accum + grad * grad
    return (param - LEARNING_RATE * grad / (jnp.sqrt(fresh) + EPSILON), fresh)


def weights(size):
    out, w = [], 1
    while w < size:
        out.append(w)
        w *= 2
    return out


class Cube:
    def __init__(self, nx, ny, split):
        gx = [("gx", w, w * ny) for w in weights(nx)]
        gy = [("gy", w, w) for w in reversed(weights(ny))]
        self.orders = [gx + gy]
        if split:
            self.orders.append(gx[:1] + gx[:0:-1] + gy)
        self.bits = len(gx) + len(gy)

    def locate(self):
        self.at = {"gx": lax.axis_index("gx"), "gy": lax.axis_index("gy")}

    def bit(self, entry):
        return (self.at[entry[0]] // entry[1]) % 2

    def partner(self, entry):
        where = dict(self.at)
        where[entry[0]] = where[entry[0]] + entry[1] * (1 - 2 * self.bit(entry))
        return (where["gx"], where["gy"])

    def greet(self):
        barrier = pltpu.get_barrier_semaphore()
        for entry in self.orders[0]:
            pl.semaphore_signal(
                barrier, inc=1, device_id=self.partner(entry), device_id_type=MESH
            )
        pl.semaphore_wait(barrier, self.bits)

    def count(self, stage):
        return 2 ** (self.bits - 1 - stage)

    def base(self, order, stage, flip):
        total = 0
        for t in range(stage + 1):
            b = self.bit(order[t])
            if flip and t == stage:
                b = 1 - b
            total = total + b * order[t][2]
        return total

    def spread(self, order, stage, i):
        free = order[stage + 1 :]
        total = 0
        for t, entry in enumerate(free):
            total += ((i >> (len(free) - 1 - t)) & 1) * entry[2]
        return total


def spread_out(cube, streams, send_sems, recv_sems):
    def copies(k, stage, flip):
        order = cube.orders[k]
        base = cube.base(order, stage, flip)
        n = cube.count(stage)
        out = []
        for i in range(n):
            block = base + cube.spread(order, stage, i)
            for m, view in enumerate(streams[k]):
                ref = view(block)
                out.append(
                    pltpu.make_async_remote_copy(
                        src_ref=ref,
                        dst_ref=ref,
                        send_sem=send_sems.at[k, m, n - 1 + i],
                        recv_sem=recv_sems.at[k, m, n - 1 + i],
                        device_id=cube.partner(order[stage]),
                        device_id_type=MESH,
                    )
                )
        return out

    for stage in range(cube.bits - 1, -1, -1):
        for k in range(len(streams)):
            if stage < cube.bits - 1:
                for c in copies(k, stage + 1, True):
                    c.wait_recv()
            for c in copies(k, stage, False):
                c.start()
    for k in range(len(streams)):
        for c in copies(k, 0, True):
            c.wait_recv()
        for stage in range(cube.bits):
            for c in copies(k, stage, False):
                c.wait_send()


def gather_kernel(cube, cot, q, r, cots, qs, rs, send_sems, recv_sems, own_sems):
    cube.locate()
    ny = lax.axis_size("gy")
    me = cube.at["gx"] * ny + cube.at["gy"]
    own = [
        pltpu.make_async_copy(src, dst.at[me], own_sems.at[m])
        for m, (src, dst) in enumerate(((cot, cots), (q, qs), (r, rs)))
    ]
    for c in own:
        c.start()
    cube.greet()
    for c in own:
        c.wait()
    half = cot.shape[0] // 2
    streams = [
        [lambda b: cots.at[b, pl.ds(0, half)], lambda b: qs.at[b]],
        [lambda b: cots.at[b, pl.ds(half, half)], lambda b: rs.at[b]],
    ]
    spread_out(cube, streams, send_sems, recv_sems)


def gather_all(nx, ny, cot, q, r):
    devices = nx * ny
    cube = Cube(nx, ny, True)
    vm = pl.BlockSpec(memory_space=VMEM)
    outs = [jax.ShapeDtypeStruct((devices,) + x.shape, x.dtype) for x in (cot, q, r)]
    return pl.pallas_call(
        functools.partial(gather_kernel, cube),
        out_shape=outs,
        in_specs=[vm] * 3,
        out_specs=[vm] * 3,
        scratch_shapes=[
            pltpu.SemaphoreType.DMA((2, 2, devices - 1)),
            pltpu.SemaphoreType.DMA((2, 2, devices - 1)),
            pltpu.SemaphoreType.DMA((3,)),
        ],
        compiler_params=pltpu.CompilerParams(collective_id=0, has_side_effects=True),
        name="gather_all",
    )(cot, q, r)


def reduce_kernel(
    cube, part, acc, fresh, update, held, sent, landed, send_sems, recv_sems, ag_send, ag_recv
):
    cube.locate()
    ny = lax.axis_size("gy")
    me = cube.at["gx"] * ny + cube.at["gy"]
    streams = len(cube.orders)
    rows = part.shape[1] // streams
    cube.greet()

    def copy(k, stage, i, src):
        slot = cube.count(stage) - 1 + i
        return pltpu.make_async_remote_copy(
            src_ref=src,
            dst_ref=landed.at[slot, pl.ds(k * rows, rows)],
            send_sem=send_sems.at[k, slot],
            recv_sem=recv_sems.at[k, slot],
            device_id=cube.partner(cube.orders[k][stage]),
            device_id_type=MESH,
        )

    def source(k, stage, i):
        if stage == 0:
            order = cube.orders[k]
            block = cube.base(order, 0, True) + cube.spread(order, 0, i)
            return part.at[block, pl.ds(k * rows, rows)]
        return sent.at[cube.count(stage) - 1 + i, pl.ds(k * rows, rows)]

    def total(k, stage, i):
        n = cube.count(stage)
        order = cube.orders[k]
        got = landed[n - 1 + i, pl.ds(k * rows, rows), :].astype(jnp.float32)
        if stage == 0:
            block = cube.base(order, 0, False) + i
            mine = part[block, pl.ds(k * rows, rows), :].astype(jnp.float32)
        else:
            mine = held[n - 1 + i, pl.ds(k * rows, rows), :]
        return mine + got

    def stage0_total(k, b, low):
        order = cube.orders[k]
        n = cube.count(0)
        half = n // 2
        got = landed[n - 1 + b * half + low, pl.ds(k * rows, rows), :]
        block = cube.base(order, 0, False) + b * order[1][2] + cube.spread(order, 1, low)
        mine = part[block, pl.ds(k * rows, rows), :]
        return mine.astype(jnp.float32) + got.astype(jnp.float32)

    for k in range(streams):
        for i in range(cube.count(0)):
            copy(k, 0, i, source(k, 0, i)).start()
    for stage in range(1, cube.bits):
        n = cube.count(stage)
        for k in range(streams):
            for i in range(2 * n):
                copy(k, stage - 1, i, source(k, stage - 1, i)).wait_recv()
            b = cube.bit(cube.orders[k][stage])

            def value(side, i, k=k, stage=stage, n=n):
                if stage == 1:
                    return stage0_total(k, side, i)
                return total(k, stage - 1, side * n + i)

            for i in range(n):
                sent[n - 1 + i, pl.ds(k * rows, rows), :] = value(1 - b, i).astype(sent.dtype)
                copy(k, stage, i, source(k, stage, i)).start()
            for i in range(n):
                held[n - 1 + i, pl.ds(k * rows, rows), :] = value(b, i)
    last = cube.bits - 1
    for k in range(streams):
        copy(k, last, 0, source(k, last, 0)).wait_recv()
        grad = total(k, last, 0)
        mine = pl.ds(k * rows, rows)
        new = acc[mine, :] + grad * grad
        fresh[mine, :] = new
        step = LEARNING_RATE * grad / (jnp.sqrt(new) + EPSILON)
        update[me, mine, :] = step.astype(update.dtype)
    views = [
        [lambda b, k=k: update.at[b, pl.ds(k * rows, rows)]] for k in range(streams)
    ]
    spread_out(cube, views, ag_send, ag_recv)
    for k in range(streams):
        for stage in range(cube.bits):
            for i in range(cube.count(stage)):
                copy(k, stage, i, source(k, stage, i)).wait_send()


def reduce_update(nx, ny, part, acc):
    devices = nx * ny
    share, width = acc.shape
    cube = Cube(nx, ny, share % 32 == 0)
    k = len(cube.orders)
    vm = pl.BlockSpec(memory_space=VMEM)
    return pl.pallas_call(
        functools.partial(reduce_kernel, cube),
        out_shape=[
            jax.ShapeDtypeStruct(acc.shape, jnp.float32),
            jax.ShapeDtypeStruct(part.shape, jnp.bfloat16),
        ],
        in_specs=[vm] * 2,
        out_specs=[vm] * 2,
        scratch_shapes=[
            pltpu.VMEM((devices // 2, share, width), jnp.float32),
            pltpu.VMEM((devices // 2, share, width), jnp.bfloat16),
            pltpu.VMEM((devices - 1, share, width), jnp.bfloat16),
            pltpu.SemaphoreType.DMA((k, devices - 1)),
            pltpu.SemaphoreType.DMA((k, devices - 1)),
            pltpu.SemaphoreType.DMA((k, 1, devices - 1)),
            pltpu.SemaphoreType.DMA((k, 1, devices - 1)),
        ],
        compiler_params=pltpu.CompilerParams(
            collective_id=1, has_side_effects=True, vmem_limit_bytes=48 * 2**20
        ),
        name="reduce_update",
    )(part, acc)


def match(ids, wanted):
    return (wanted[:, None] == ids[None, :]).astype(jnp.bfloat16)


def local(
    quotient_table,
    quotient_acc,
    remainder_table,
    remainder_acc,
    cotangent,
    quotient_ids,
    remainder_ids,
    nx,
    ny,
):
    devices = nx * ny
    q_dev, width = quotient_table.shape
    r_rows = remainder_table.shape[0]
    share = remainder_acc.shape[0]
    samples, bag = quotient_ids.shape
    count = samples * bag
    capacity = max(2, (2 * count + devices - 1) // devices)
    slots = devices * capacity
    f32, bf16 = jnp.float32, jnp.bfloat16
    me = lax.axis_index(("gx", "gy"))
    cots, qs, rs = gather_all(
        nx, ny, cotangent, quotient_ids.reshape(1, count), remainder_ids.reshape(1, count)
    )
    qs = qs.reshape(devices, count)
    rs = rs.reshape(devices, count)
    near = qs - me * q_dev
    mine = (near >= 0) & (near < q_dev)
    steps = jnp.arange(count, dtype=jnp.int32)
    before = (steps[:, None] < steps[None, :]).astype(bf16)
    place = jnp.dot(mine.astype(bf16), before, preferred_element_type=f32)
    place = jnp.where(mine, place, -1.0).astype(jnp.int32)
    seat = jnp.arange(capacity, dtype=jnp.int32)
    pick = (place[:, None, :] == seat[None, :, None]).astype(bf16)
    near = jnp.where(mine, near, 0)
    sample = jnp.broadcast_to(steps // bag + 1, (devices, count))
    facts = jnp.stack(
        [near // 256, near % 256, rs // 256, rs % 256, sample // 128, sample % 128], axis=1
    ).astype(bf16)
    told = jnp.einsum("nvk,nck->vnc", facts, pick, preferred_element_type=f32).astype(jnp.int32)
    row = (told[0] * 256 + told[1]).reshape(slots)
    rem = (told[2] * 256 + told[3]).reshape(slots)
    who = told[4] * 128 + told[5]
    whose = (who[:, :, None] == 1 + jnp.arange(samples, dtype=jnp.int32)).astype(bf16)
    cot_rows = jnp.einsum("ncs,nsw->ncw", whose, cots, preferred_element_type=f32)
    cot_rows = cot_rows.reshape(slots, width)
    rem_rows = lax.optimization_barrier(remainder_table[rem].astype(bf16))
    wanted = jnp.arange(q_dev, dtype=jnp.int32)
    q_rows = jnp.dot(
        (row[:, None] == wanted[None, :]).astype(bf16),
        quotient_table.astype(bf16),
        preferred_element_type=f32,
    )
    q_terms = (cot_rows * rem_rows.astype(f32)).astype(bf16)
    r_terms = (cot_rows * q_rows).astype(bf16)
    part = jnp.dot(
        match(rem, jnp.arange(r_rows, dtype=jnp.int32)), r_terms, preferred_element_type=f32
    ).astype(bf16)
    new_remainder_acc, update = reduce_update(
        nx, ny, part.reshape(devices, share, width), remainder_acc
    )
    quotient_grad = jnp.dot(match(row, wanted), q_terms, preferred_element_type=f32)
    new_quotient, new_quotient_acc = adagrad(quotient_table, quotient_acc, quotient_grad)
    new_remainder = remainder_table - update.reshape(r_rows, width).astype(f32)
    return (new_quotient, new_quotient_acc, new_remainder, new_remainder_acc)


def solution(mesh):
    rows = P(("gx", "gy"), None)
    return jax.shard_map(
        functools.partial(local, nx=mesh.shape["gx"], ny=mesh.shape["gy"]),
        mesh=mesh,
        in_specs=(rows, rows, P(), rows, rows, rows, rows),
        out_specs=(rows, rows, P(), rows),
        check_vma=False,
    )
```

```python
import functools

import jax
import jax.numpy as jnp
from jax import lax
from jax.experimental import pallas as pl
from jax.experimental.pallas import tpu as pltpu
from jax.sharding import PartitionSpec as P

LEARNING_RATE = 0.1
EPSILON = 1e-10
MESH = pl.DeviceIdType.MESH
VMEM = pltpu.VMEM


def adagrad(param, accum, grad):
    fresh = accum + grad * grad
    return (param - LEARNING_RATE * grad / (jnp.sqrt(fresh) + EPSILON), fresh)


def weights(size):
    out, w = [], 1
    while w < size:
        out.append(w)
        w *= 2
    return out


class Cube:
    def __init__(self, nx, ny, rows):
        gx = [("gx", w, w * ny) for w in weights(nx)]
        gy = [("gy", w, w) for w in weights(ny)]
        orders = [gx + gy, gx[:1] + gx[:0:-1] + gy, gx[:1] + gy + gx[1:]]
        self.bits = len(gx) + len(gy)
        self.orders, self.spans = [], []
        units = rows // 16
        last = max(1, units // 4) if units >= 3 and rows % 16 == 0 else 0
        if units < 2 or rows % 16:
            sizes = [rows]
        else:
            sizes = [16 * ((units - last + 1) // 2), 16 * ((units - last) // 2), 16 * last]
        start = 0
        for order, size in zip(orders, sizes):
            if size:
                self.orders.append(order)
                self.spans.append((start, size))
                start += size
        self.streams = len(self.orders)

    def locate(self):
        self.at = {"gx": lax.axis_index("gx"), "gy": lax.axis_index("gy")}

    def bit(self, entry):
        return (self.at[entry[0]] // entry[1]) % 2

    def partner(self, entry):
        where = dict(self.at)
        where[entry[0]] = where[entry[0]] + entry[1] * (1 - 2 * self.bit(entry))
        return (where["gx"], where["gy"])

    def greet(self):
        barrier = pltpu.get_barrier_semaphore()
        for entry in self.orders[0]:
            pl.semaphore_signal(
                barrier, inc=1, device_id=self.partner(entry), device_id_type=MESH
            )
        pl.semaphore_wait(barrier, self.bits)

    def count(self, stage):
        return 2 ** (self.bits - 1 - stage)

    def free(self, k, stage):
        return sorted(self.orders[k][stage + 1 :], key=lambda e: -e[2])

    def run(self, k, stage):
        g = 1
        for entry in reversed(self.free(k, stage)):
            if entry[2] != g:
                break
            g *= 2
        return g

    def base(self, k, stage, flip):
        order = self.orders[k]
        total = 0
        for t in range(stage + 1):
            b = self.bit(order[t])
            if flip and t == stage:
                b = 1 - b
            total = total + b * order[t][2]
        return total

    def spread(self, k, stage, i):
        total = 0
        for t, entry in enumerate(reversed(self.free(k, stage))):
            total += ((i >> t) & 1) * entry[2]
        return total

    def child(self, k, stage, i):
        free = self.free(k, stage - 1)
        p = len(free) - 1 - free.index(self.orders[k][stage])
        return ((i >> p) << (p + 1)) | (i & (2**p - 1)), 2**p


def spread_out(cube, streams, send_sems, recv_sems, between=lambda stage: None):
    def copies(k, stage, flip):
        base = cube.base(k, stage, flip)
        n, g = cube.count(stage), cube.run(k, stage)
        out = []
        for i in range(0, n, g):
            block = base + cube.spread(k, stage, i)
            for m, view in enumerate(streams[k]):
                ref = view(pl.ds(block, g))
                out.append(
                    pltpu.make_async_remote_copy(
                        src_ref=ref,
                        dst_ref=ref,
                        send_sem=send_sems.at[k, m, n - 1 + i],
                        recv_sem=recv_sems.at[k, m, n - 1 + i],
                        device_id=cube.partner(cube.orders[k][stage]),
                        device_id_type=MESH,
                    )
                )
        return out

    for stage in range(cube.bits - 1, -1, -1):
        for k in range(len(streams)):
            if stage < cube.bits - 1:
                for c in copies(k, stage + 1, True):
                    c.wait_recv()
            for c in copies(k, stage, False):
                c.start()
        between(stage)
    for k in range(len(streams)):
        for c in copies(k, 0, True):
            c.wait_recv()
        for stage in range(cube.bits):
            for c in copies(k, stage, False):
                c.wait_send()


def gather_kernel(cube, cot, q, r, cots, qs, rs, send_sems, recv_sems, own_sems):
    cube.locate()
    ny = lax.axis_size("gy")
    me = cube.at["gx"] * ny + cube.at["gy"]
    own = [
        pltpu.make_async_copy(src, dst.at[me], own_sems.at[m])
        for m, (src, dst) in enumerate(((cot, cots), (q, qs), (r, rs)))
    ]
    for c in own:
        c.start()
    cube.greet()
    for c in own:
        c.wait()
    streams = [
        [lambda b, lo=lo, size=size: cots.at[b, pl.ds(lo, size)]] for lo, size in cube.spans
    ]
    streams[-1].append(lambda b: qs.at[b])
    streams[-2 % cube.streams].append(lambda b: rs.at[b])
    spread_out(cube, streams, send_sems, recv_sems)


def gather_all(nx, ny, cot, q, r):
    devices = nx * ny
    cube = Cube(nx, ny, cot.shape[0])
    vm = pl.BlockSpec(memory_space=VMEM)
    outs = [jax.ShapeDtypeStruct((devices,) + x.shape, x.dtype) for x in (cot, q, r)]
    return pl.pallas_call(
        functools.partial(gather_kernel, cube),
        out_shape=outs,
        in_specs=[vm] * 3,
        out_specs=[vm] * 3,
        scratch_shapes=[
            pltpu.SemaphoreType.DMA((cube.streams, 3, devices - 1)),
            pltpu.SemaphoreType.DMA((cube.streams, 3, devices - 1)),
            pltpu.SemaphoreType.DMA((3,)),
        ],
        compiler_params=pltpu.CompilerParams(collective_id=0, has_side_effects=True),
        name="gather_all",
    )(cot, q, r)


def reduce_kernel(
    cube, part, acc, fresh, update, held, sent, landed, send_sems, recv_sems, ag_send, ag_recv
):
    cube.locate()
    ny = lax.axis_size("gy")
    me = cube.at["gx"] * ny + cube.at["gy"]
    cube.greet()

    def rows(k):
        return pl.ds(*cube.spans[k])

    def copy(k, stage, i):
        n, g = cube.count(stage), cube.run(k, stage)
        if stage == 0:
            src = part.at[pl.ds(cube.base(k, 0, True) + cube.spread(k, 0, i), g), rows(k)]
        else:
            src = sent.at[pl.ds(n - 1 + i, g), rows(k)]
        return pltpu.make_async_remote_copy(
            src_ref=src,
            dst_ref=landed.at[pl.ds(n - 1 + i, g), rows(k)],
            send_sem=send_sems.at[k, n - 1 + i],
            recv_sem=recv_sems.at[k, n - 1 + i],
            device_id=cube.partner(cube.orders[k][stage]),
            device_id_type=MESH,
        )

    def copies(k, stage):
        return [copy(k, stage, i) for i in range(0, cube.count(stage), cube.run(k, stage))]

    def value(k, stage, side, i):
        n = cube.count(stage - 1)
        start, step = cube.child(k, stage, i)
        at = n - 1 + start + side * step
        got = landed[at, rows(k), :].astype(jnp.float32)
        if stage == 1:
            block = cube.base(k, 0, False) + cube.spread(k, 0, start)
            block = block + side * cube.orders[k][1][2]
            return part[block, rows(k), :].astype(jnp.float32) + got
        return held[at, rows(k), :] + got

    for k in range(cube.streams):
        for c in copies(k, 0):
            c.start()
    for stage in range(1, cube.bits):
        n = cube.count(stage)
        for k in range(cube.streams):
            for c in copies(k, stage - 1):
                c.wait_recv()
            b = cube.bit(cube.orders[k][stage])
            g = cube.run(k, stage)
            for i in range(n):
                sent[n - 1 + i, rows(k), :] = value(k, stage, 1 - b, i).astype(sent.dtype)
                if (i + 1) % g == 0:
                    copy(k, stage, i + 1 - g).start()
            for i in range(n):
                held[n - 1 + i, rows(k), :] = value(k, stage, b, i)
    last = cube.bits - 1
    for k in range(cube.streams):
        copy(k, last, 0).wait_recv()
        grad = held[0, rows(k), :] + landed[0, rows(k), :].astype(jnp.float32)
        new = acc[rows(k), :] + grad * grad
        fresh[rows(k), :] = new
        step = LEARNING_RATE * grad / (jnp.sqrt(new) + EPSILON)
        update[me, rows(k), :] = step.astype(update.dtype)
    views = [[lambda b, k=k: update.at[b, rows(k)]] for k in range(cube.streams)]
    spread_out(cube, views, ag_send, ag_recv)
    for k in range(cube.streams):
        for stage in range(cube.bits):
            for c in copies(k, stage):
                c.wait_send()


def reduce_update(nx, ny, part, acc):
    devices = nx * ny
    share, width = acc.shape
    cube = Cube(nx, ny, share)
    k = cube.streams
    vm = pl.BlockSpec(memory_space=VMEM)
    return pl.pallas_call(
        functools.partial(reduce_kernel, cube),
        out_shape=[
            jax.ShapeDtypeStruct(acc.shape, jnp.float32),
            jax.ShapeDtypeStruct(part.shape, jnp.bfloat16),
        ],
        in_specs=[vm] * 2,
        out_specs=[vm] * 2,
        scratch_shapes=[
            pltpu.VMEM((devices // 2, share, width), jnp.float32),
            pltpu.VMEM((devices // 2, share, width), jnp.bfloat16),
            pltpu.VMEM((devices - 1, share, width), jnp.bfloat16),
            pltpu.SemaphoreType.DMA((k, devices - 1)),
            pltpu.SemaphoreType.DMA((k, devices - 1)),
            pltpu.SemaphoreType.DMA((k, 1, devices - 1)),
            pltpu.SemaphoreType.DMA((k, 1, devices - 1)),
        ],
        compiler_params=pltpu.CompilerParams(
            collective_id=1, has_side_effects=True, vmem_limit_bytes=48 * 2**20
        ),
        name="reduce_update",
    )(part, acc)


def match(ids, wanted):
    return (wanted[:, None] == ids[None, :]).astype(jnp.bfloat16)


def local(
    quotient_table,
    quotient_acc,
    remainder_table,
    remainder_acc,
    cotangent,
    quotient_ids,
    remainder_ids,
    nx,
    ny,
):
    devices = nx * ny
    q_dev, width = quotient_table.shape
    r_rows = remainder_table.shape[0]
    share = remainder_acc.shape[0]
    samples, bag = quotient_ids.shape
    count = samples * bag
    capacity = max(2, (2 * count + devices - 1) // devices)
    slots = devices * capacity
    f32, bf16 = jnp.float32, jnp.bfloat16
    me = lax.axis_index(("gx", "gy"))
    cots, qs, rs = gather_all(
        nx, ny, cotangent, quotient_ids.T.reshape(1, count), remainder_ids.T.reshape(1, count)
    )
    qs = qs.reshape(devices, count)
    rs = rs.reshape(devices, count)
    near = qs - me * q_dev
    mine = (near >= 0) & (near < q_dev)
    steps = jnp.arange(count, dtype=jnp.int32)
    before = (steps[:, None] < steps[None, :]).astype(bf16)
    place = jnp.dot(mine.astype(bf16), before, preferred_element_type=f32)
    place = jnp.where(mine, place, -1.0).astype(jnp.int32)
    seat = jnp.arange(capacity, dtype=jnp.int32)
    pick = (place[:, None, :] == seat[None, :, None]).astype(bf16)
    near = jnp.where(mine, near, 0)
    sample = jnp.broadcast_to(steps % samples + 1, (devices, count))
    facts = jnp.stack(
        [near // 256, near % 256, rs // 256, rs % 256, sample // 128, sample % 128], axis=1
    ).astype(bf16)
    told = jnp.einsum("nvk,nck->vnc", facts, pick, preferred_element_type=f32).astype(jnp.int32)
    row = (told[0] * 256 + told[1]).reshape(slots)
    rem = (told[2] * 256 + told[3]).reshape(slots)
    who = told[4] * 128 + told[5]
    whose = (who[:, :, None] == 1 + jnp.arange(samples, dtype=jnp.int32)).astype(bf16)
    cot_rows = jnp.einsum("ncs,nsw->ncw", whose, cots, preferred_element_type=f32)
    cot_rows = cot_rows.reshape(slots, width)
    rem_rows = lax.optimization_barrier(remainder_table[rem].astype(bf16))
    wanted = jnp.arange(q_dev, dtype=jnp.int32)
    q_rows = jnp.dot(
        (row[:, None] == wanted[None, :]).astype(bf16),
        quotient_table.astype(bf16),
        preferred_element_type=f32,
    )
    q_terms = (cot_rows * rem_rows.astype(f32)).astype(bf16)
    r_terms = (cot_rows * q_rows).astype(bf16)
    r_terms = lax.optimization_barrier(r_terms)
    tile = 256 if r_rows % 256 == 0 else r_rows
    tiles = jnp.arange(r_rows // tile, dtype=jnp.int32)
    inside = rem[None, :] - tile * tiles[:, None]
    inside = jnp.where((inside >= 0) & (inside < tile), inside, -1).astype(bf16)
    inside = lax.optimization_barrier(inside)
    offset = jnp.arange(tile, dtype=jnp.int32).astype(bf16)
    hit = (inside[:, None, :] == offset[None, :, None]).astype(bf16)
    part = jnp.einsum("tis,sw->tiw", hit, r_terms, preferred_element_type=f32).astype(bf16)
    new_remainder_acc, update = reduce_update(
        nx, ny, part.reshape(devices, share, width), remainder_acc
    )
    quotient_grad = jnp.dot(match(row, wanted), q_terms, preferred_element_type=f32)
    new_quotient, new_quotient_acc = adagrad(quotient_table, quotient_acc, quotient_grad)
    new_remainder = remainder_table - update.reshape(r_rows, width).astype(f32)
    return (new_quotient, new_quotient_acc, new_remainder, new_remainder_acc)


def solution(mesh):
    rows = P(("gx", "gy"), None)
    return jax.shard_map(
        functools.partial(local, nx=mesh.shape["gx"], ny=mesh.shape["gy"]),
        mesh=mesh,
        in_specs=(rows, rows, P(), rows, rows, rows, rows),
        out_specs=(rows, rows, P(), rows),
        check_vma=False,
    )
```

```python
import functools

import jax
import jax.numpy as jnp
from jax import lax
from jax.experimental import pallas as pl
from jax.experimental.pallas import tpu as pltpu
from jax.sharding import PartitionSpec as P

LEARNING_RATE = 0.1
EPSILON = 1e-10
MESH = pl.DeviceIdType.MESH
VMEM = pltpu.VMEM


def adagrad(param, accum, grad):
    fresh = accum + grad * grad
    return (param - LEARNING_RATE * grad / (jnp.sqrt(fresh) + EPSILON), fresh)


def weights(size):
    out, w = [], 1
    while w < size:
        out.append(w)
        w *= 2
    return out


class Cube:
    def __init__(self, nx, ny, rows):
        gx = [("gx", w, w * ny) for w in weights(nx)]
        gy = [("gy", w, w) for w in weights(ny)]
        orders = [gx + gy, gx[:1] + gx[:0:-1] + gy, gx[:1] + gy + gx[1:]]
        self.bits = len(gx) + len(gy)
        self.orders, self.spans = [], []
        units = rows // 16
        last = max(1, units // 4) if units >= 3 and rows % 16 == 0 else 0
        if units < 2 or rows % 16:
            sizes = [rows]
        else:
            sizes = [16 * ((units - last + 1) // 2), 16 * ((units - last) // 2), 16 * last]
        start = 0
        for order, size in zip(orders, sizes):
            if size:
                self.orders.append(order)
                self.spans.append((start, size))
                start += size
        self.streams = len(self.orders)

    def locate(self):
        self.at = {"gx": lax.axis_index("gx"), "gy": lax.axis_index("gy")}

    def bit(self, entry):
        return (self.at[entry[0]] // entry[1]) % 2

    def partner(self, entry):
        where = dict(self.at)
        where[entry[0]] = where[entry[0]] + entry[1] * (1 - 2 * self.bit(entry))
        return (where["gx"], where["gy"])

    def greet(self):
        barrier = pltpu.get_barrier_semaphore()
        for entry in self.orders[0]:
            pl.semaphore_signal(
                barrier, inc=1, device_id=self.partner(entry), device_id_type=MESH
            )
        pl.semaphore_wait(barrier, self.bits)

    def count(self, stage):
        return 2 ** (self.bits - 1 - stage)

    def free(self, k, stage):
        return sorted(self.orders[k][stage + 1 :], key=lambda e: -e[2])

    def run(self, k, stage):
        g = 1
        for entry in reversed(self.free(k, stage)):
            if entry[2] != g:
                break
            g *= 2
        return g

    def base(self, k, stage, flip):
        order = self.orders[k]
        total = 0
        for t in range(stage + 1):
            b = self.bit(order[t])
            if flip and t == stage:
                b = 1 - b
            total = total + b * order[t][2]
        return total

    def spread(self, k, stage, i):
        total = 0
        for t, entry in enumerate(reversed(self.free(k, stage))):
            total += ((i >> t) & 1) * entry[2]
        return total

    def child(self, k, stage, i):
        free = self.free(k, stage - 1)
        p = len(free) - 1 - free.index(self.orders[k][stage])
        return ((i >> p) << (p + 1)) | (i & (2**p - 1)), 2**p


def spread_out(cube, streams, send_sems, recv_sems, between=lambda stage: None):
    def copies(k, stage, flip):
        base = cube.base(k, stage, flip)
        n, g = cube.count(stage), cube.run(k, stage)
        out = []
        for i in range(0, n, g):
            block = base + cube.spread(k, stage, i)
            for m, view in enumerate(streams[k]):
                ref = view(pl.ds(block, g))
                out.append(
                    pltpu.make_async_remote_copy(
                        src_ref=ref,
                        dst_ref=ref,
                        send_sem=send_sems.at[k, m, n - 1 + i],
                        recv_sem=recv_sems.at[k, m, n - 1 + i],
                        device_id=cube.partner(cube.orders[k][stage]),
                        device_id_type=MESH,
                    )
                )
        return out

    for stage in range(cube.bits - 1, -1, -1):
        for k in range(len(streams)):
            if stage < cube.bits - 1:
                for c in copies(k, stage + 1, True):
                    c.wait_recv()
            for c in copies(k, stage, False):
                c.start()
        between(stage)
    for k in range(len(streams)):
        for c in copies(k, 0, True):
            c.wait_recv()
        for stage in range(cube.bits):
            for c in copies(k, stage, False):
                c.wait_send()


def gather_kernel(cube, cot, q, r, cots, qs, rs, send_sems, recv_sems, own_sems):
    cube.locate()
    ny = lax.axis_size("gy")
    me = cube.at["gx"] * ny + cube.at["gy"]
    own = [
        pltpu.make_async_copy(src, dst.at[me], own_sems.at[m])
        for m, (src, dst) in enumerate(((cot, cots), (q, qs), (r, rs)))
    ]
    for c in own:
        c.start()
    cube.greet()
    for c in own:
        c.wait()
    streams = [
        [lambda b, lo=lo, size=size: cots.at[b, pl.ds(lo, size)]] for lo, size in cube.spans
    ]
    streams[-1].append(lambda b: qs.at[b])
    streams[-2 % cube.streams].append(lambda b: rs.at[b])
    spread_out(cube, streams, send_sems, recv_sems)


def gather_all(nx, ny, cot, q, r):
    devices = nx * ny
    cube = Cube(nx, ny, cot.shape[0])
    vm = pl.BlockSpec(memory_space=VMEM)
    outs = [jax.ShapeDtypeStruct((devices,) + x.shape, x.dtype) for x in (cot, q, r)]
    return pl.pallas_call(
        functools.partial(gather_kernel, cube),
        out_shape=outs,
        in_specs=[vm] * 3,
        out_specs=[vm] * 3,
        scratch_shapes=[
            pltpu.SemaphoreType.DMA((cube.streams, 3, devices - 1)),
            pltpu.SemaphoreType.DMA((cube.streams, 3, devices - 1)),
            pltpu.SemaphoreType.DMA((3,)),
        ],
        compiler_params=pltpu.CompilerParams(collective_id=0, has_side_effects=True),
        name="gather_all",
    )(cot, q, r)


def reduce_kernel(
    cube,
    part,
    acc,
    table,
    rem,
    row,
    cot_rows,
    fresh,
    update,
    grads,
    held,
    sent,
    landed,
    wide,
    narrow,
    send_sems,
    recv_sems,
    ag_send,
    ag_recv,
    table_sem,
):
    fetch = pltpu.make_async_copy(table, wide, table_sem)
    fetch.start()

    cube.locate()
    ny = lax.axis_size("gy")
    me = cube.at["gx"] * ny + cube.at["gy"]
    cube.greet()

    def rows(k):
        return pl.ds(*cube.spans[k])

    def copy(k, stage, i):
        n, g = cube.count(stage), cube.run(k, stage)
        if stage == 0:
            src = part.at[pl.ds(cube.base(k, 0, True) + cube.spread(k, 0, i), g), rows(k)]
        else:
            src = sent.at[pl.ds(n - 1 + i, g), rows(k)]
        return pltpu.make_async_remote_copy(
            src_ref=src,
            dst_ref=landed.at[pl.ds(n - 1 + i, g), rows(k)],
            send_sem=send_sems.at[k, n - 1 + i],
            recv_sem=recv_sems.at[k, n - 1 + i],
            device_id=cube.partner(cube.orders[k][stage]),
            device_id_type=MESH,
        )

    def copies(k, stage):
        return [copy(k, stage, i) for i in range(0, cube.count(stage), cube.run(k, stage))]

    def value(k, stage, side, i):
        n = cube.count(stage - 1)
        start, step = cube.child(k, stage, i)
        at = n - 1 + start + side * step
        got = landed[at, rows(k), :].astype(jnp.float32)
        if stage == 1:
            block = cube.base(k, 0, False) + cube.spread(k, 0, start)
            block = block + side * cube.orders[k][1][2]
            return part[block, rows(k), :].astype(jnp.float32) + got
        return held[at, rows(k), :] + got

    slots = rem.shape[0]
    piece = 256 if slots % 256 == 0 else slots
    pieces = slots // piece
    gaps = 2 * cube.bits

    def quotient_piece(p):
        at = pl.ds(p * piece, piece)
        names = lax.broadcasted_iota(jnp.int32, (piece, table.shape[0]), 1)
        pick = (names == rem[at, :]).astype(jnp.bfloat16)
        found = jnp.dot(pick, narrow[...], preferred_element_type=jnp.float32)
        terms = (cot_rows[at, :].astype(jnp.float32) * found).astype(jnp.bfloat16)
        names = lax.broadcasted_iota(jnp.int32, (grads.shape[0], piece), 0)
        spot = (names == row[:, at]).astype(jnp.bfloat16)
        sums = jnp.dot(spot, terms, preferred_element_type=jnp.float32)
        if p == 0:
            grads[...] = sums
        else:
            grads[...] += sums

    def gap(g):
        for p in range(g * pieces // gaps, (g + 1) * pieces // gaps):
            quotient_piece(p)

    for k in range(cube.streams):
        for c in copies(k, 0):
            c.start()
    fetch.wait()
    narrow[...] = wide[...].astype(jnp.bfloat16)
    gap(0)
    for stage in range(1, cube.bits):
        n = cube.count(stage)
        for k in range(cube.streams):
            for c in copies(k, stage - 1):
                c.wait_recv()
            b = cube.bit(cube.orders[k][stage])
            g = cube.run(k, stage)
            for i in range(n):
                sent[n - 1 + i, rows(k), :] = value(k, stage, 1 - b, i).astype(sent.dtype)
                if (i + 1) % g == 0:
                    copy(k, stage, i + 1 - g).start()
            for i in range(n):
                held[n - 1 + i, rows(k), :] = value(k, stage, b, i)
        gap(stage)
    last = cube.bits - 1
    for k in range(cube.streams):
        copy(k, last, 0).wait_recv()
        grad = held[0, rows(k), :] + landed[0, rows(k), :].astype(jnp.float32)
        new = acc[rows(k), :] + grad * grad
        fresh[rows(k), :] = new
        step = LEARNING_RATE * grad / (jnp.sqrt(new) + EPSILON)
        update[me, rows(k), :] = step.astype(update.dtype)
    views = [[lambda b, k=k: update.at[b, rows(k)]] for k in range(cube.streams)]
    spread_out(cube, views, ag_send, ag_recv, lambda stage: gap(gaps - 1 - stage))
    for k in range(cube.streams):
        for stage in range(cube.bits):
            for c in copies(k, stage):
                c.wait_send()


def reduce_update(nx, ny, part, acc, table, rem, row, cot_rows, q_dev):
    devices = nx * ny
    share, width = acc.shape
    cube = Cube(nx, ny, share)
    k = cube.streams
    vm = pl.BlockSpec(memory_space=VMEM)
    return pl.pallas_call(
        functools.partial(reduce_kernel, cube),
        out_shape=[
            jax.ShapeDtypeStruct(acc.shape, jnp.float32),
            jax.ShapeDtypeStruct(part.shape, jnp.bfloat16),
            jax.ShapeDtypeStruct((q_dev, width), jnp.float32),
        ],
        in_specs=[vm, vm, pl.BlockSpec(memory_space=pl.ANY), vm, vm, vm],
        out_specs=[vm] * 3,
        scratch_shapes=[
            pltpu.VMEM((devices // 2, share, width), jnp.float32),
            pltpu.VMEM((devices // 2, share, width), jnp.bfloat16),
            pltpu.VMEM((devices - 1, share, width), jnp.bfloat16),
            pltpu.VMEM(table.shape, jnp.float32),
            pltpu.VMEM(table.shape, jnp.bfloat16),
            pltpu.SemaphoreType.DMA((k, devices - 1)),
            pltpu.SemaphoreType.DMA((k, devices - 1)),
            pltpu.SemaphoreType.DMA((k, 1, devices - 1)),
            pltpu.SemaphoreType.DMA((k, 1, devices - 1)),
            pltpu.SemaphoreType.DMA,
        ],
        compiler_params=pltpu.CompilerParams(
            collective_id=1, has_side_effects=True, vmem_limit_bytes=48 * 2**20
        ),
        name="reduce_update",
    )(part, acc, table, rem, row, cot_rows)


def local(
    quotient_table,
    quotient_acc,
    remainder_table,
    remainder_acc,
    cotangent,
    quotient_ids,
    remainder_ids,
    nx,
    ny,
):
    devices = nx * ny
    q_dev, width = quotient_table.shape
    r_rows = remainder_table.shape[0]
    share = remainder_acc.shape[0]
    samples, bag = quotient_ids.shape
    count = samples * bag
    capacity = max(2, (2 * count + devices - 1) // devices)
    slots = devices * capacity
    f32, bf16 = jnp.float32, jnp.bfloat16
    me = lax.axis_index(("gx", "gy"))
    cots, qs, rs = gather_all(
        nx, ny, cotangent, quotient_ids.T.reshape(1, count), remainder_ids.T.reshape(1, count)
    )
    qs = qs.reshape(devices, count)
    rs = rs.reshape(devices, count)
    near = qs - me * q_dev
    mine = (near >= 0) & (near < q_dev)
    steps = jnp.arange(count, dtype=jnp.int32)
    before = (steps[:, None] < steps[None, :]).astype(bf16)
    place = jnp.dot(mine.astype(bf16), before, preferred_element_type=f32)
    place = jnp.where(mine, place, -1.0).astype(jnp.int32)
    seat = jnp.arange(capacity, dtype=jnp.int32)
    pick = (place[:, None, :] == seat[None, :, None]).astype(bf16)
    near = jnp.where(mine, near, 0)
    sample = jnp.broadcast_to(steps % samples + 1, (devices, count))
    facts = jnp.stack(
        [near // 256, near % 256, rs // 256, rs % 256, sample // 128, sample % 128], axis=1
    ).astype(bf16)
    told = jnp.einsum("nvk,nck->vnc", facts, pick, preferred_element_type=f32).astype(jnp.int32)
    row = (told[0] * 256 + told[1]).reshape(slots)
    rem = (told[2] * 256 + told[3]).reshape(slots)
    who = told[4] * 128 + told[5]
    whose = (who[:, :, None] == 1 + jnp.arange(samples, dtype=jnp.int32)).astype(bf16)
    cot_rows = jnp.einsum("ncs,nsw->ncw", whose, cots, preferred_element_type=f32)
    cot_rows = cot_rows.reshape(slots, width)
    wanted = jnp.arange(q_dev, dtype=jnp.int32)
    q_rows = jnp.dot(
        (row[:, None] == wanted[None, :]).astype(bf16),
        quotient_table.astype(bf16),
        preferred_element_type=f32,
    )
    r_terms = (cot_rows * q_rows).astype(bf16)
    r_terms = lax.optimization_barrier(r_terms)
    tile = 256 if r_rows % 256 == 0 else r_rows
    tiles = jnp.arange(r_rows // tile, dtype=jnp.int32)
    inside = rem[None, :] - tile * tiles[:, None]
    inside = jnp.where((inside >= 0) & (inside < tile), inside, -1).astype(bf16)
    inside = lax.optimization_barrier(inside)
    offset = jnp.arange(tile, dtype=jnp.int32).astype(bf16)
    hit = (inside[:, None, :] == offset[None, :, None]).astype(bf16)
    part = jnp.einsum("tis,sw->tiw", hit, r_terms, preferred_element_type=f32).astype(bf16)
    new_remainder_acc, update, quotient_grad = reduce_update(
        nx,
        ny,
        part.reshape(devices, share, width),
        remainder_acc,
        remainder_table,
        rem.reshape(slots, 1),
        row.reshape(1, slots),
        cot_rows.astype(bf16),
        q_dev,
    )
    new_quotient, new_quotient_acc = adagrad(quotient_table, quotient_acc, quotient_grad)
    new_remainder = remainder_table - update.reshape(r_rows, width).astype(f32)
    return (new_quotient, new_quotient_acc, new_remainder, new_remainder_acc)


def solution(mesh):
    rows = P(("gx", "gy"), None)
    return jax.shard_map(
        functools.partial(local, nx=mesh.shape["gx"], ny=mesh.shape["gy"]),
        mesh=mesh,
        in_specs=(rows, rows, P(), rows, rows, rows, rows),
        out_specs=(rows, rows, P(), rows),
        check_vma=False,
    )
```

```python
import functools

import jax
import jax.numpy as jnp
from jax import lax
from jax.experimental import pallas as pl
from jax.experimental.pallas import tpu as pltpu
from jax.sharding import PartitionSpec as P

LEARNING_RATE = 0.1
EPSILON = 1e-10
MESH = pl.DeviceIdType.MESH
VMEM = pltpu.VMEM


def adagrad(param, accum, grad):
    fresh = accum + grad * grad
    return (param - LEARNING_RATE * grad / (jnp.sqrt(fresh) + EPSILON), fresh)


def weights(size):
    out, w = [], 1
    while w < size:
        out.append(w)
        w *= 2
    return out


class Cube:
    def __init__(self, nx, ny, rows):
        gx = [("gx", w, w * ny) for w in weights(nx)]
        gy = [("gy", w, w) for w in weights(ny)]
        orders = [gx + gy, gx[:1] + gx[:0:-1] + gy, gx[:1] + gy + gx[1:]]
        self.bits = len(gx) + len(gy)
        self.orders, self.spans = [], []
        units = rows // 16
        last = max(1, units // 4) if units >= 3 and rows % 16 == 0 else 0
        if units < 2 or rows % 16:
            sizes = [rows]
        else:
            sizes = [16 * ((units - last + 1) // 2), 16 * ((units - last) // 2), 16 * last]
        start = 0
        for order, size in zip(orders, sizes):
            if size:
                self.orders.append(order)
                self.spans.append((start, size))
                start += size
        self.streams = len(self.orders)

    def locate(self):
        self.at = {"gx": lax.axis_index("gx"), "gy": lax.axis_index("gy")}

    def bit(self, entry):
        return (self.at[entry[0]] // entry[1]) % 2

    def partner(self, entry):
        where = dict(self.at)
        where[entry[0]] = where[entry[0]] + entry[1] * (1 - 2 * self.bit(entry))
        return (where["gx"], where["gy"])

    def greet(self):
        barrier = pltpu.get_barrier_semaphore()
        for entry in self.orders[0]:
            pl.semaphore_signal(
                barrier, inc=1, device_id=self.partner(entry), device_id_type=MESH
            )
        pl.semaphore_wait(barrier, self.bits)

    def count(self, stage):
        return 2 ** (self.bits - 1 - stage)

    def free(self, k, stage):
        return sorted(self.orders[k][stage + 1 :], key=lambda e: -e[2])

    def run(self, k, stage):
        g = 1
        for entry in reversed(self.free(k, stage)):
            if entry[2] != g:
                break
            g *= 2
        return g

    def base(self, k, stage, flip):
        order = self.orders[k]
        total = 0
        for t in range(stage + 1):
            b = self.bit(order[t])
            if flip and t == stage:
                b = 1 - b
            total = total + b * order[t][2]
        return total

    def spread(self, k, stage, i):
        total = 0
        for t, entry in enumerate(reversed(self.free(k, stage))):
            total += ((i >> t) & 1) * entry[2]
        return total

    def child(self, k, stage, i):
        free = self.free(k, stage - 1)
        p = len(free) - 1 - free.index(self.orders[k][stage])
        return ((i >> p) << (p + 1)) | (i & (2**p - 1)), 2**p


def spread_out(cube, streams, send_sems, recv_sems, between=lambda stage: None):
    def copies(k, stage, flip):
        base = cube.base(k, stage, flip)
        n, g = cube.count(stage), cube.run(k, stage)
        out = []
        for i in range(0, n, g):
            block = base + cube.spread(k, stage, i)
            for m, view in enumerate(streams[k]):
                ref = view(pl.ds(block, g))
                out.append(
                    pltpu.make_async_remote_copy(
                        src_ref=ref,
                        dst_ref=ref,
                        send_sem=send_sems.at[k, m, n - 1 + i],
                        recv_sem=recv_sems.at[k, m, n - 1 + i],
                        device_id=cube.partner(cube.orders[k][stage]),
                        device_id_type=MESH,
                    )
                )
        return out

    for stage in range(cube.bits - 1, -1, -1):
        for k in range(len(streams)):
            if stage < cube.bits - 1:
                for c in copies(k, stage + 1, True):
                    c.wait_recv()
            for c in copies(k, stage, False):
                c.start()
        between(stage)
    for k in range(len(streams)):
        for c in copies(k, 0, True):
            c.wait_recv()
        for stage in range(cube.bits):
            for c in copies(k, stage, False):
                c.wait_send()


def gather_kernel(cube, cot, q, r, cots, qs, rs, send_sems, recv_sems, own_sems):
    cube.locate()
    ny = lax.axis_size("gy")
    me = cube.at["gx"] * ny + cube.at["gy"]
    own = [
        pltpu.make_async_copy(src, dst.at[me], own_sems.at[m])
        for m, (src, dst) in enumerate(((cot, cots), (q, qs), (r, rs)))
    ]
    for c in own:
        c.start()
    cube.greet()
    for c in own:
        c.wait()
    streams = [
        [lambda b, lo=lo, size=size: cots.at[b, pl.ds(lo, size)]] for lo, size in cube.spans
    ]
    streams[-1].append(lambda b: qs.at[b])
    streams[-2 % cube.streams].append(lambda b: rs.at[b])
    spread_out(cube, streams, send_sems, recv_sems)


def gather_all(nx, ny, cot, q, r):
    devices = nx * ny
    cube = Cube(nx, ny, cot.shape[0])
    vm = pl.BlockSpec(memory_space=VMEM)
    outs = [jax.ShapeDtypeStruct((devices,) + x.shape, x.dtype) for x in (cot, q, r)]
    return pl.pallas_call(
        functools.partial(gather_kernel, cube),
        out_shape=outs,
        in_specs=[vm] * 3,
        out_specs=[vm] * 3,
        scratch_shapes=[
            pltpu.SemaphoreType.DMA((cube.streams, 3, devices - 1)),
            pltpu.SemaphoreType.DMA((cube.streams, 3, devices - 1)),
            pltpu.SemaphoreType.DMA((3,)),
        ],
        compiler_params=pltpu.CompilerParams(
            collective_id=0, has_side_effects=True, vmem_limit_bytes=8 * 2**20
        ),
        name="gather_all",
    )(cot, q, r)


def reduce_kernel(
    cube,
    part,
    acc,
    table,
    rem,
    row,
    cot_rows,
    fresh,
    update,
    grads,
    held,
    sent,
    landed,
    wide,
    narrow,
    send_sems,
    recv_sems,
    ag_send,
    ag_recv,
    table_sem,
):
    fetch = pltpu.make_async_copy(table, wide, table_sem)
    fetch.start()

    cube.locate()
    ny = lax.axis_size("gy")
    me = cube.at["gx"] * ny + cube.at["gy"]
    cube.greet()

    def rows(k):
        return pl.ds(*cube.spans[k])

    def copy(k, stage, i):
        n, g = cube.count(stage), cube.run(k, stage)
        if stage == 0:
            src = part.at[pl.ds(cube.base(k, 0, True) + cube.spread(k, 0, i), g), rows(k)]
        else:
            src = sent.at[pl.ds(n - 1 + i, g), rows(k)]
        return pltpu.make_async_remote_copy(
            src_ref=src,
            dst_ref=landed.at[pl.ds(n - 1 + i, g), rows(k)],
            send_sem=send_sems.at[k, n - 1 + i],
            recv_sem=recv_sems.at[k, n - 1 + i],
            device_id=cube.partner(cube.orders[k][stage]),
            device_id_type=MESH,
        )

    def copies(k, stage):
        return [copy(k, stage, i) for i in range(0, cube.count(stage), cube.run(k, stage))]

    def value(k, stage, side, i):
        n = cube.count(stage - 1)
        start, step = cube.child(k, stage, i)
        at = n - 1 + start + side * step
        got = landed[at, rows(k), :].astype(jnp.float32)
        if stage == 1:
            block = cube.base(k, 0, False) + cube.spread(k, 0, start)
            block = block + side * cube.orders[k][1][2]
            return part[block, rows(k), :].astype(jnp.float32) + got
        return held[at, rows(k), :] + got

    slots = rem.shape[0]
    piece = 256 if slots % 256 == 0 else slots
    pieces = slots // piece
    gaps = 2 * cube.bits

    def quotient_piece(p):
        at = pl.ds(p * piece, piece)
        names = lax.broadcasted_iota(jnp.int32, (piece, table.shape[0]), 1)
        pick = (names == rem[at, :]).astype(jnp.bfloat16)
        found = jnp.dot(pick, narrow[...], preferred_element_type=jnp.float32)
        terms = (cot_rows[at, :].astype(jnp.float32) * found).astype(jnp.bfloat16)
        names = lax.broadcasted_iota(jnp.int32, (grads.shape[0], piece), 0)
        spot = (names == row[:, at]).astype(jnp.bfloat16)
        sums = jnp.dot(spot, terms, preferred_element_type=jnp.float32)
        if p == 0:
            grads[...] = sums
        else:
            grads[...] += sums

    def gap(g):
        for p in range(g * pieces // gaps, (g + 1) * pieces // gaps):
            quotient_piece(p)

    for k in range(cube.streams):
        for c in copies(k, 0):
            c.start()
    fetch.wait()
    narrow[...] = wide[...].astype(jnp.bfloat16)
    gap(0)
    for stage in range(1, cube.bits):
        n = cube.count(stage)
        for k in range(cube.streams):
            for c in copies(k, stage - 1):
                c.wait_recv()
            b = cube.bit(cube.orders[k][stage])
            g = cube.run(k, stage)
            for i in range(n):
                sent[n - 1 + i, rows(k), :] = value(k, stage, 1 - b, i).astype(sent.dtype)
                if (i + 1) % g == 0:
                    copy(k, stage, i + 1 - g).start()
            for i in range(n):
                held[n - 1 + i, rows(k), :] = value(k, stage, b, i)
        gap(stage)
    last = cube.bits - 1
    for k in range(cube.streams):
        copy(k, last, 0).wait_recv()
        grad = held[0, rows(k), :] + landed[0, rows(k), :].astype(jnp.float32)
        new = acc[rows(k), :] + grad * grad
        fresh[rows(k), :] = new
        step = LEARNING_RATE * grad / (jnp.sqrt(new) + EPSILON)
        update[me, rows(k), :] = step.astype(update.dtype)
    views = [[lambda b, k=k: update.at[b, rows(k)]] for k in range(cube.streams)]
    spread_out(cube, views, ag_send, ag_recv, lambda stage: gap(gaps - 1 - stage))
    for k in range(cube.streams):
        for stage in range(cube.bits):
            for c in copies(k, stage):
                c.wait_send()


def reduce_update(nx, ny, part, acc, table, rem, row, cot_rows, q_dev):
    devices = nx * ny
    share, width = acc.shape
    cube = Cube(nx, ny, share)
    k = cube.streams
    vm = pl.BlockSpec(memory_space=VMEM)
    return pl.pallas_call(
        functools.partial(reduce_kernel, cube),
        out_shape=[
            jax.ShapeDtypeStruct(acc.shape, jnp.float32),
            jax.ShapeDtypeStruct(part.shape, jnp.bfloat16),
            jax.ShapeDtypeStruct((q_dev, width), jnp.float32),
        ],
        in_specs=[vm, vm, pl.BlockSpec(memory_space=pl.ANY), vm, vm, vm],
        out_specs=[vm] * 3,
        scratch_shapes=[
            pltpu.VMEM((devices // 2, share, width), jnp.float32),
            pltpu.VMEM((devices // 2, share, width), jnp.bfloat16),
            pltpu.VMEM((devices - 1, share, width), jnp.bfloat16),
            pltpu.VMEM(table.shape, jnp.float32),
            pltpu.VMEM(table.shape, jnp.bfloat16),
            pltpu.SemaphoreType.DMA((k, devices - 1)),
            pltpu.SemaphoreType.DMA((k, devices - 1)),
            pltpu.SemaphoreType.DMA((k, 1, devices - 1)),
            pltpu.SemaphoreType.DMA((k, 1, devices - 1)),
            pltpu.SemaphoreType.DMA,
        ],
        compiler_params=pltpu.CompilerParams(
            collective_id=1, has_side_effects=True, vmem_limit_bytes=28 * 2**20
        ),
        name="reduce_update",
    )(part, acc, table, rem, row, cot_rows)


def local(
    quotient_table,
    quotient_acc,
    remainder_table,
    remainder_acc,
    cotangent,
    quotient_ids,
    remainder_ids,
    nx,
    ny,
):
    devices = nx * ny
    q_dev, width = quotient_table.shape
    r_rows = remainder_table.shape[0]
    share = remainder_acc.shape[0]
    samples, bag = quotient_ids.shape
    count = samples * bag
    capacity = max(2, (2 * count + devices - 1) // devices)
    slots = devices * capacity
    f32, bf16 = jnp.float32, jnp.bfloat16
    me = lax.axis_index(("gx", "gy"))
    cots, qs, rs = gather_all(
        nx, ny, cotangent, quotient_ids.T.reshape(1, count), remainder_ids.T.reshape(1, count)
    )
    qs = qs.reshape(devices, count)
    rs = rs.reshape(devices, count)
    near = qs - me * q_dev
    mine = (near >= 0) & (near < q_dev)
    steps = jnp.arange(count, dtype=jnp.int32)
    before = (steps[:, None] < steps[None, :]).astype(bf16)
    place = jnp.dot(mine.astype(bf16), before, preferred_element_type=f32)
    place = jnp.where(mine, place, -1.0).astype(jnp.int32)
    seat = jnp.arange(capacity, dtype=jnp.int32)
    pick = (place[:, None, :] == seat[None, :, None]).astype(bf16)
    near = jnp.where(mine, near, 0)
    sample = jnp.broadcast_to(steps % samples + 1, (devices, count))
    facts = jnp.stack(
        [near // 256, near % 256, rs // 256, rs % 256, sample // 128, sample % 128], axis=1
    ).astype(bf16)
    told = jnp.einsum("nvk,nck->vnc", facts, pick, preferred_element_type=f32).astype(jnp.int32)
    row = (told[0] * 256 + told[1]).reshape(slots)
    rem = (told[2] * 256 + told[3]).reshape(slots)
    who = told[4] * 128 + told[5]
    whose = (who[:, :, None] == 1 + jnp.arange(samples, dtype=jnp.int32)).astype(bf16)
    cot_rows = jnp.einsum("ncs,nsw->ncw", whose, cots, preferred_element_type=f32)
    cot_rows = cot_rows.reshape(slots, width)
    wanted = jnp.arange(q_dev, dtype=jnp.int32)
    q_rows = jnp.dot(
        (row[:, None] == wanted[None, :]).astype(bf16),
        quotient_table.astype(bf16),
        preferred_element_type=f32,
    )
    r_terms = (cot_rows * q_rows).astype(bf16)
    r_terms = lax.optimization_barrier(r_terms)
    tile = 256 if r_rows % 256 == 0 else r_rows
    tiles = jnp.arange(r_rows // tile, dtype=jnp.int32)
    inside = rem[None, :] - tile * tiles[:, None]
    inside = jnp.where((inside >= 0) & (inside < tile), inside, -1).astype(bf16)
    inside = lax.optimization_barrier(inside)
    offset = jnp.arange(tile, dtype=jnp.int32).astype(bf16)
    hit = (inside[:, None, :] == offset[None, :, None]).astype(bf16)
    part = jnp.einsum("tis,sw->tiw", hit, r_terms, preferred_element_type=f32).astype(bf16)
    new_remainder_acc, update, quotient_grad = reduce_update(
        nx,
        ny,
        part.reshape(devices, share, width),
        remainder_acc,
        remainder_table,
        rem.reshape(slots, 1),
        row.reshape(1, slots),
        cot_rows.astype(bf16),
        q_dev,
    )
    new_quotient, new_quotient_acc = adagrad(quotient_table, quotient_acc, quotient_grad)
    new_remainder = remainder_table - update.reshape(r_rows, width).astype(f32)
    return (new_quotient, new_quotient_acc, new_remainder, new_remainder_acc)


def solution(mesh):
    rows = P(("gx", "gy"), None)
    return jax.shard_map(
        functools.partial(local, nx=mesh.shape["gx"], ny=mesh.shape["gy"]),
        mesh=mesh,
        in_specs=(rows, rows, P(), rows, rows, rows, rows),
        out_specs=(rows, rows, P(), rows),
        check_vma=False,
    )
```
